32 devices in a mesh: section: 4 (over x, core), dp: 8 (over z, y).
Axes of the slice: x: 2, y: 2, z: 4, core: 2. Of those that a mesh axis runs over, the one named last changes fastest.
Arguments:
- token_ids: int32 [2, 16], P(None, 'dp'), may hold values from 0 to 8191
- target_ids: int32 [2, 16], P(None, 'dp'), may hold values from 0 to 8191
- table: bfloat16 [8192, 4608], P(('section', 'dp')), may hold values from -0.06629126 to 0.06629126
- norm_gain: bfloat16 [2, 4, 4608], P(None, 'section'), may hold values from 0.099609375 to 1.8984375
- w_in: bfloat16 [2, 4, 8, 4608], P(None, 'section'), may hold values from -0.09375 to 0.09375
- w_out: bfloat16 [2, 4, 8, 4608], P(None, 'section'), may hold values from -2 to 2
- final_gain: bfloat16 [4608], replicated, may hold values from 0.099609375 to 1.8984375
Outputs:
- token_loss: float32 [2, 16], P(None, 'dp')
- table_grad: bfloat16 [8192, 4608], P(('section', 'dp'))
The draws below stay inside these ranges and needn't reach their ends.
All inputs are finite; a program needn't handle non-finite values.
Results may differ from the reference program's by a relative error of at most 0.013.
The reference program's roundings to bfloat16 on the way (of `embedded`, `final_rows`, `head_input`, `score_grad`, `final_grad` and `embedded_grad`) count: a program that leaves them out, or rounds other values in their place, can miss the bound.
Values may be sent and summed in bfloat16 or wider, within the bound.
A program may use at most 64 MiB of HBM per device.

```python
import math
import jax
import jax.numpy as jnp
import numpy as np
from jax import lax

D = 4608
RANK = 8
V_DEV = 256
M = 2
VOCAB = 8192
TOKENS = 16
N_SECTION = 4


def draw_table(key, part):
    direction_key, level_key, jitter_key, noise_key = jax.random.split(key, 4)
    row_scale = 0.55 / D ** 0.5
    regions = VOCAB // V_DEV
    direction = jnp.clip(jax.random.normal(direction_key, (D,), jnp.float32), -2.5, 2.5)
    levels = jax.random.uniform(level_key, (regions,), jnp.float32, 0.5, 1.5)
    noise_part = jnp.clip(jax.random.normal(noise_key, (VOCAB, D), jnp.float32), -3.5, 3.5)
    jitter = jax.random.uniform(jitter_key, (VOCAB,), jnp.float32, 0.8, 1.2)
    loading = jnp.broadcast_to(levels[:, None], (regions, V_DEV)).reshape(VOCAB) * jitter
    return (row_scale * (loading[:, None] * direction[None, :] + noise_part)).astype(jnp.bfloat16)


def place_ends(array, stream_key, smallest, high):
    dims = array.shape
    index_at = [jax.random.randint(jax.random.fold_in(stream_key, axis), (), 0, dims[axis]) for axis in range(len(dims))]
    array = array.at[tuple(index_at)].set(smallest)
    longest = dims.index(max(dims))
    index_at[longest] = (index_at[longest] + 1) % dims[longest]
    return array.at[tuple(index_at)].set(high)


def block_levels(rng, dims, pieces, least, top_value):
    level, own = 1.0, jax.random.fold_in(rng, 6)
    for axis_at, shards_of in pieces:
        draws = jnp.exp(jax.random.uniform(jax.random.fold_in(own, axis_at), (shards_of,), jnp.float32, least / len(pieces), top_value / len(pieces)))
        level = level * jnp.repeat(draws, dims[axis_at] // shards_of).reshape([-1 if axis == axis_at else 1 for axis in range(len(dims))])
    return level


def rank_bounds(count, slope):
    loads = [(1 << 20) // math.isqrt(rank ** slope) + 1 for rank in range(1, count + 1)]
    deviation = 1 + sum(loads) // (1 << 30)
    return np.cumsum(np.array([max(1, weight // deviation) for weight in loads]))


def ranked(rng, dims, number_of, lean):
    grid = rank_bounds(number_of, lean)
    pick = jax.random.randint(jax.random.fold_in(rng, 1), dims, 0, int(grid[number_of - 1]))
    grade = jnp.searchsorted(jnp.asarray(grid, jnp.int32), pick, side="right")
    return jax.random.permutation(jax.random.fold_in(rng, 2), number_of)[grade].astype(jnp.int32)


def gaussian(key, extent, scale, most, cuts=(), kind=jnp.bfloat16):
    drawn = scale * jax.random.normal(key, extent, jnp.float32)
    if cuts:
        drawn = drawn * block_levels(key, extent, cuts, -0.22, 0.18)
    return jnp.clip(drawn, -most, most).astype(kind)


def setup_inputs(seed: int = 0) -> dict:
    keys = jax.random.split(jax.random.key(seed), 8)
    token_ids = place_ends(ranked(keys[0], (M, TOKENS), VOCAB, 2), jax.random.fold_in(keys[0], 3), 0, VOCAB - 1).astype(jnp.int32)
    target_ids = place_ends(ranked(keys[1], (M, TOKENS), VOCAB, 2), jax.random.fold_in(keys[1], 3), 0, VOCAB - 1).astype(jnp.int32)
    table = draw_table(jax.random.fold_in(keys[7], 71), 0)
    norm_gain = jnp.clip(1.0 + 0.18 * jax.random.normal(keys[3], (2, N_SECTION, D), jnp.float32), 0.099609375, 1.8984375).astype(jnp.bfloat16)
    w_in = gaussian(keys[4], (2, N_SECTION, RANK, D), D ** -0.5, 0.09375, ((1, 4),))
    w_out = gaussian(keys[5], (2, N_SECTION, RANK, D), RANK ** -0.5, 2.0, ((1, 4),))
    final_gain = jnp.clip(1.0 + 0.18 * jax.random.normal(keys[6], (D,), jnp.float32), 0.099609375, 1.8984375).astype(jnp.bfloat16)
    return dict(token_ids=token_ids, target_ids=target_ids, table=table, norm_gain=norm_gain, w_in=w_in, w_out=w_out, final_gain=final_gain)


EPS = 1e-06
CAP = 30.0
GELU_C = 0.7978845608028654

def gelu_tanh(values):
    return 0.5 * values * (1.0 + jnp.tanh(GELU_C * (values + 0.044715 * values * values * values)))

def gelu_slope(values):
    inner = jnp.tanh(GELU_C * (values + 0.044715 * values * values * values))
    return 0.5 * (1.0 + inner) + 0.5 * values * (1.0 - inner * inner) * GELU_C * (1.0 + 3.0 * 0.044715 * values * values)

def normalize(rows_in):
    values = rows_in.astype(jnp.float32)
    scale = lax.rsqrt(lax.optimization_barrier(jnp.mean(values * values, axis=-1, keepdims=True)) + EPS)
    return (values * scale, scale)

def norm_back(normed, scale, grad):
    return scale * (grad - normed * lax.optimization_barrier(jnp.mean(grad * normed, axis=-1, keepdims=True)))

def layer_forward(rows_in, gain, first_proj, second_proj):
    normed, scale = normalize(rows_in)
    activated = (normed * gain.astype(jnp.float32)).astype(jnp.bfloat16)
    preact = lax.dot_general(activated, first_proj, (((1,), (1,)), ((), ())), preferred_element_type=jnp.float32)
    hidden = gelu_tanh(preact).astype(jnp.bfloat16)
    branch = jnp.dot(hidden, second_proj, preferred_element_type=jnp.float32)
    return (rows_in.astype(jnp.float32) + branch).astype(jnp.bfloat16)

def layer_backward(rows_in, gain, first_proj, second_proj, grad_out):
    normed, scale = normalize(rows_in)
    gain_float = gain.astype(jnp.float32)
    activated = (normed * gain_float).astype(jnp.bfloat16)
    preact = lax.dot_general(activated, first_proj, (((1,), (1,)), ((), ())), preferred_element_type=jnp.float32)
    hidden_grad = lax.dot_general(grad_out, second_proj, (((1,), (1,)), ((), ())), preferred_element_type=jnp.float32)
    preact_grad = (hidden_grad * gelu_slope(preact)).astype(jnp.bfloat16)
    act_grad = jnp.dot(preact_grad, first_proj, preferred_element_type=jnp.float32)
    return (grad_out.astype(jnp.float32) + norm_back(normed, scale, act_grad * gain_float)).astype(jnp.bfloat16)

def reference(token_ids, target_ids, table, norm_gain, w_in, w_out, final_gain):
    layer_total = 2 * N_SECTION
    layer_gains = norm_gain.reshape(layer_total, D)
    weights_in = w_in.reshape(layer_total, RANK, D)
    weights_out = w_out.reshape(layer_total, RANK, D)
    embed_scale = math.sqrt(D)
    final_scale = final_gain.astype(jnp.float32)
    vocab_index = jnp.arange(VOCAB, dtype=jnp.int32)

    def one_batch(carry, batch_item):
        input_list, goal_list = batch_item
        embedded = (table[input_list].astype(jnp.float32) * embed_scale).astype(jnp.bfloat16)

        def forward_layer(current, layer_params):
            gain, first_proj, second_proj = layer_params
            return (layer_forward(current, gain, first_proj, second_proj), current)
        final_rows, stored = lax.scan(forward_layer, embedded, (layer_gains, weights_in, weights_out))
        normed, scale = normalize(final_rows)
        head_input = (normed * final_scale).astype(jnp.bfloat16)
        scores = lax.dot_general(head_input, table, (((1,), (1,)), ((), ())), preferred_element_type=jnp.float32)
        squash = jnp.tanh(scores / CAP)
        capped = CAP * squash
        powers = jnp.exp(capped)
        exp_total = lax.optimization_barrier(jnp.sum(powers, axis=1))
        target_mask = goal_list[:, None] == vocab_index[None, :]
        target_score = lax.optimization_barrier(jnp.sum(jnp.where(target_mask, capped, jnp.float32(0.0)), axis=1))
        token_loss = jnp.log(exp_total) - target_score
        score_grad = ((powers / exp_total[:, None] - target_mask.astype(jnp.float32)) * (1.0 - squash * squash)).astype(jnp.bfloat16)
        head_input_grad = jnp.dot(score_grad, table, preferred_element_type=jnp.float32)
        final_grad = norm_back(normed, scale, head_input_grad * final_scale).astype(jnp.bfloat16)

        def backward_layer(grad_now, layer_params):
            rows_in, gain, first_proj, second_proj = layer_params
            return (layer_backward(rows_in, gain, first_proj, second_proj, grad_now), None)
        embedded_grad, _ = lax.scan(backward_layer, final_grad, (stored, layer_gains, weights_in, weights_out), reverse=True)
        return (carry, (token_loss, score_grad, head_input, embedded_grad))
    start = jnp.zeros((), jnp.float32)
    _, outputs = lax.scan(one_batch, start, (token_ids, target_ids))
    losses, score_grads, head_inputs, embedded_grads = outputs
    head_part = lax.dot_general(score_grads.reshape(-1, VOCAB), head_inputs.reshape(-1, D), (((0,), (0,)), ((), ())), preferred_element_type=jnp.float32)
    table_grad = head_part.at[token_ids.reshape(-1)].add(embedded_grads.reshape(-1, D).astype(jnp.float32) * embed_scale)
    return (losses, table_grad.astype(jnp.bfloat16))
```

```python
import math

import jax
import jax.numpy as jnp
from jax import lax
from jax.sharding import PartitionSpec as P

EPS = 1e-06
CAP = 30.0
GELU_C = 0.7978845608028654


def shifted(block, axis, distance):
    devices = range(lax.axis_size(axis))
    route = [((i - distance) % len(devices), i) for i in devices]
    return lax.ppermute(block, axis, route)


def from_root(block, axis, source):
    block = jnp.where(lax.axis_index(axis) == source, block, jnp.zeros_like(block))
    return lax.psum(block, axis)


def gelu_tanh(values):
    return 0.5 * values * (1.0 + jnp.tanh(GELU_C * (values + 0.044715 * values * values * values)))


def gelu_slope(values):
    inner = jnp.tanh(GELU_C * (values + 0.044715 * values * values * values))
    return 0.5 * (1.0 + inner) + 0.5 * values * (1.0 - inner * inner) * GELU_C * (
        1.0 + 3.0 * 0.044715 * values * values
    )


def normalize(rows_in):
    values = rows_in.astype(jnp.float32)
    scale = lax.rsqrt(jnp.mean(values * values, axis=-1, keepdims=True) + EPS)
    return (values * scale, scale)


def norm_back(normed, scale, grad):
    return scale * (grad - normed * jnp.mean(grad * normed, axis=-1, keepdims=True))


def layer_forward(rows_in, gain, first_proj, second_proj):
    normed, scale = normalize(rows_in)
    activated = (normed * gain.astype(jnp.float32)).astype(jnp.bfloat16)
    preact = lax.dot_general(
        activated, first_proj, (((1,), (1,)), ((), ())), preferred_element_type=jnp.float32
    )
    hidden = gelu_tanh(preact).astype(jnp.bfloat16)
    branch = jnp.dot(hidden, second_proj, preferred_element_type=jnp.float32)
    return (rows_in.astype(jnp.float32) + branch).astype(jnp.bfloat16)


def layer_backward(rows_in, gain, first_proj, second_proj, grad_out):
    normed, scale = normalize(rows_in)
    gain_float = gain.astype(jnp.float32)
    activated = (normed * gain_float).astype(jnp.bfloat16)
    preact = lax.dot_general(
        activated, first_proj, (((1,), (1,)), ((), ())), preferred_element_type=jnp.float32
    )
    hidden_grad = lax.dot_general(
        grad_out, second_proj, (((1,), (1,)), ((), ())), preferred_element_type=jnp.float32
    )
    preact_grad = (hidden_grad * gelu_slope(preact)).astype(jnp.bfloat16)
    act_grad = jnp.dot(preact_grad, first_proj, preferred_element_type=jnp.float32)
    return (grad_out.astype(jnp.float32) + norm_back(normed, scale, act_grad * gain_float)).astype(
        jnp.bfloat16
    )


def per_device(token_ids, target_ids, table, norm_gain, w_in, w_out, final_gain):
    sections = lax.axis_size("section")
    section_index = lax.axis_index("section")
    replicas = lax.axis_size("dp")
    replica_index = lax.axis_index("dp")
    batches, width = token_ids.shape
    rows_dev, dim = table.shape
    embed_scale = math.sqrt(dim)
    offset = (section_index * replicas + replica_index) * rows_dev
    columns = jnp.arange(rows_dev, dtype=jnp.int32)
    final_scale = final_gain.astype(jnp.float32)
    ids = lax.all_gather(jnp.concatenate([token_ids, target_ids], 0), "dp", axis=1, tiled=True)
    gains = lax.all_gather(norm_gain, "section", axis=1, tiled=True).reshape(-1, dim)
    first = lax.all_gather(w_in, "section", axis=1, tiled=True).reshape(
        2 * sections, -1, dim
    )
    second = lax.all_gather(w_out, "section", axis=1, tiled=True).reshape(
        2 * sections, -1, dim
    )
    all_inputs, all_targets = ids[:batches], ids[batches:]
    wide = all_inputs.shape[1]
    token_count = batches * wide
    chosen = ((all_inputs.reshape(token_count) - offset)[:, None] == columns[None, :]).astype(
        jnp.bfloat16
    )
    looked = jnp.dot(chosen, table, preferred_element_type=jnp.float32).astype(jnp.bfloat16)
    looked = lax.psum(looked, ("section", "dp")).astype(jnp.float32)
    rows = (looked * embed_scale).astype(jnp.bfloat16)

    def forward(rows, weights):
        return layer_forward(rows, *weights), rows

    rows, inputs = lax.scan(forward, rows, (gains, first, second))
    normed, scale = normalize(rows)
    head_input = (normed * final_scale).astype(jnp.bfloat16)
    scores = lax.dot_general(
        head_input, table, (((1,), (1,)), ((), ())), preferred_element_type=jnp.float32
    )
    squash = jnp.tanh(scores / CAP)
    capped = CAP * squash
    powers = jnp.exp(capped)
    goal_local = all_targets.reshape(token_count) - offset
    target_mask = goal_local[:, None] == columns[None, :]
    stats = lax.psum(
        jnp.stack(
            [
                jnp.sum(powers, axis=1),
                jnp.sum(jnp.where(target_mask, capped, jnp.float32(0.0)), axis=1),
            ]
        ),
        ("section", "dp"),
    )
    exp_total, target_score = stats[0], stats[1]
    loss_all = (jnp.log(exp_total) - target_score).reshape(batches, wide)
    token_loss = lax.dynamic_slice_in_dim(loss_all, replica_index * width, width, 1)
    score_grad = (
        (powers / exp_total[:, None] - target_mask.astype(jnp.float32)) * (1.0 - squash * squash)
    ).astype(jnp.bfloat16)
    partial_value = jnp.dot(score_grad, table, preferred_element_type=jnp.float32)
    head_in_grad = lax.psum(partial_value, ("section", "dp"))
    grad = norm_back(normed, scale, head_in_grad * final_scale).astype(jnp.bfloat16)

    def backward(grad, saved):
        return layer_backward(*saved, grad), None

    grad, _ = lax.scan(backward, grad, (inputs, gains, first, second), reverse=True)
    head_grad = lax.dot_general(
        score_grad, head_input, (((0,), (0,)), ((), ())), preferred_element_type=jnp.float32
    )
    embed_grad = (
        lax.dot_general(chosen, grad, (((0,), (0,)), ((), ())), preferred_element_type=jnp.float32)
        * embed_scale
    )
    return (token_loss, (head_grad + embed_grad).astype(jnp.bfloat16))


def solution(mesh):
    return jax.shard_map(
        per_device,
        mesh=mesh,
        in_specs=(
            P(None, "dp"),
            P(None, "dp"),
            P(("section", "dp"), None),
            P(None, "section", None),
            P(None, "section", None, None),
            P(None, "section", None, None),
            P(),
        ),
        out_specs=(P(None, "dp"), P(("section", "dp"), None)),
        check_vma=False,
    )
```

```python
import functools
import math

import jax
import jax.numpy as jnp
from jax import lax
from jax.experimental import pallas as pl
from jax.experimental.pallas import tpu as pltpu
from jax.sharding import PartitionSpec as P

EPS = 1e-06
CAP = 30.0
GELU_C = 0.7978845608028654
LANES = 128
F32 = jnp.float32
BF16 = jnp.bfloat16
IDS, GAIN, WIN, WOUT, LOOK, HEAD, STAT, GRAD, EMB = range(9)


def gelu_tanh(values):
    return 0.5 * values * (1.0 + jnp.tanh(GELU_C * (values + 0.044715 * values * values * values)))


def gelu_slope(values):
    inner = jnp.tanh(GELU_C * (values + 0.044715 * values * values * values))
    return 0.5 * (1.0 + inner) + 0.5 * values * (1.0 - inner * inner) * GELU_C * (
        1.0 + 3.0 * 0.044715 * values * values
    )


def rounded(values):
    return values.astype(BF16).astype(F32)


def cascade(
    sections, replicas, per_dp, pad,
    ids_ref, table_ref, gain_ref, win_ref, wout_ref, fgain_ref,
    loss_ref, sg_ref, chosen_ref, head_ref, emb_ref,
    idbuf, idrow, gains, wins, wouts, flat, look_out, look_in, tok, layer_in,
    head_out, head_in, stat_out, stat_in, grad_out, grad_in, emb_out, emb_in,
    send_sem, recv_sem,
):
    devices = sections * replicas
    tokens = replicas * per_dp
    rows_dev, dim = table_ref.shape
    chunks = dim // LANES
    layers = 2 * sections
    scale_in = math.sqrt(dim)
    sec, rep = lax.axis_index("section"), lax.axis_index("dp")
    me = sec * replicas + rep
    offset = me * rows_dev
    all_own = per_dp == sections
    own = sec < per_dp
    my_token = rep * per_dp + sec if all_own else jnp.where(own, rep * per_dp + sec, -1)

    def if_own(body):
        if all_own:
            body()
        else:
            pl.when(own)(body)

    def spread(phase, count, first, target, skip, src, dst):
        def step(i, _):
            at = lax.rem(first + i, count)

            @pl.when(at != skip)
            def _():
                pltpu.make_async_remote_copy(
                    src_ref=src(at),
                    dst_ref=dst,
                    send_sem=send_sem.at[phase],
                    recv_sem=recv_sem.at[phase],
                    device_id=target(at),
                    device_id_type=pl.DeviceIdType.MESH,
                ).start()

            @pl.when(at == skip)
            def _():
                pltpu.make_async_copy(src(at), dst, recv_sem.at[phase]).start()

            return 0

        lax.fori_loop(0, count, step, 0)

    def take(ref, sem):
        pltpu.make_async_copy(ref, ref, sem).wait()

    def any_device(n):
        return (n // replicas, n % replicas)

    def token_device(t):
        return (t % per_dp, t // per_dp)

    barrier = pltpu.get_barrier_semaphore()

    def greet(i, _):
        n = lax.rem(me + 1 + i, devices)
        pl.semaphore_signal(
            barrier, inc=1, device_id=any_device(n), device_id_type=pl.DeviceIdType.MESH
        )
        return 0

    lax.fori_loop(0, devices - 1, greet, 0)
    flat[...] = jnp.zeros_like(flat)
    tok[...] = jnp.zeros_like(tok)
    pl.semaphore_wait(barrier, devices - 1)

    spread(IDS, replicas, rep, lambda d: (sec, d), rep, lambda d: ids_ref, idbuf.at[rep])
    for phase, src, dst in ((GAIN, gain_ref, gains), (WIN, win_ref, wins), (WOUT, wout_ref, wouts)):
        spread(
            phase, sections, sec, lambda s: (s, rep), sec, lambda s, src=src: src, dst.at[sec]
        )

    take(idbuf, recv_sem.at[IDS])
    for d in range(replicas):
        for kind in range(2):
            for k in range(per_dp):
                idrow[kind, pl.ds(d * per_dp + k, 1), :] = idbuf[
                    d, pl.ds(kind * per_dp + k, 1), :
                ]
    wide = lambda value: jnp.concatenate([value] * (rows_dev // LANES), axis=1)
    column = lax.broadcasted_iota(jnp.int32, (tokens, rows_dev), 1) + offset
    chosen = jnp.where(wide(idrow[0]) == column, 1.0, 0.0).astype(BF16)
    mask = wide(idrow[1]) == column
    chosen_ref[...] = chosen

    def scatter(left, phase, out, into):
        for j in range(0, chunks, 2):
            part = jnp.dot(
                left, table_ref[:, j * LANES : (j + 2) * LANES], preferred_element_type=F32
            )
            flat[pl.ds(j, tokens, stride=pad), :] = part[:, :LANES]
            flat[pl.ds(j + 1, tokens, stride=pad), :] = part[:, LANES:]
        out[...] = flat[...].astype(BF16).reshape(tokens, pad, LANES)
        spread(
            phase, tokens, rep * per_dp + sec, token_device, my_token,
            lambda t: out.at[t], into.at[me],
        )

    def total(into):
        return lax.fori_loop(
            0, devices, lambda n, acc: acc + into[n].astype(F32), jnp.zeros((pad, LANES), F32)
        )

    def spread_rows(values):
        tok[...] = values
        return jnp.concatenate(
            [jnp.broadcast_to(tok[j : j + 1, :], (8, LANES)) for j in range(chunks)], axis=1
        )

    def pack_row(values, out):
        for j in range(chunks):
            tok[j : j + 1, :] = values[0:1, j * LANES : (j + 1) * LANES]
        out[...] = tok[...].astype(BF16)

    def norm(x):
        scale = lax.rsqrt(jnp.sum(x * x, axis=1, keepdims=True) * (1.0 / dim) + EPS)
        return x * scale, scale

    def weights(layer):
        s, c = layer % sections, layer // sections
        return (
            spread_rows(gains[s, c].astype(F32)),
            wins[s, c].astype(F32),
            wouts[s, c].astype(F32),
        )

    def gather(phase, block, into):
        if_own(
            lambda: spread(
                phase, devices, me, any_device, me, lambda n: block, into.at[my_token]
            )
        )

    def unpack(into, out):
        flat[...] = into[...].reshape(tokens * pad, LANES).astype(F32)
        for j in range(chunks):
            out[:, j * LANES : (j + 1) * LANES] = flat[
                pl.ds(j, tokens, stride=pad), :
            ].astype(BF16)

    scatter(chosen, LOOK, look_out, look_in)
    take(gains, recv_sem.at[GAIN])
    take(wins, recv_sem.at[WIN])
    take(wouts, recv_sem.at[WOUT])

    def forward():
        take(look_in, recv_sem.at[LOOK])
        x = spread_rows(rounded(total(look_in) * scale_in))

        def layer(index, x):
            layer_in[index] = x
            gain, first, second = weights(index)
            normed, _ = norm(x)
            pre = jnp.sum(rounded(normed * gain) * first, axis=1, keepdims=True)
            hidden = rounded(gelu_tanh(pre))
            return rounded(x + jnp.sum(hidden * second, axis=0, keepdims=True))

        x = lax.fori_loop(0, layers, layer, x)
        layer_in[layers] = x
        normed, _ = norm(x)
        pack_row(normed * spread_rows(fgain_ref[...].astype(F32)), head_out)

    if_own(forward)
    gather(HEAD, head_out, head_in)
    take(head_in, recv_sem.at[HEAD])
    unpack(head_in, head_ref)

    scores = lax.dot_general(
        head_ref[...], table_ref[...], (((1,), (1,)), ((), ())), preferred_element_type=F32
    )
    squash = jnp.tanh(scores / CAP)
    capped = CAP * squash
    powers = jnp.exp(capped)
    exp_sum = jnp.sum(powers, axis=1, keepdims=True)
    goal = jnp.sum(jnp.where(mask, capped, 0.0), axis=1, keepdims=True)
    groups = tokens // 8
    lane = lax.broadcasted_iota(jnp.int32, (8, LANES), 1)
    tile = jnp.zeros((8, LANES), F32)
    for g in range(groups):
        tile = jnp.where(lane == g, exp_sum[8 * g : 8 * g + 8], tile)
        tile = jnp.where(lane == groups + g, goal[8 * g : 8 * g + 8], tile)
    stat_out[...] = tile
    spread(STAT, devices, me, any_device, me, lambda n: stat_out, stat_in.at[me])
    take(stat_in, recv_sem.at[STAT])
    tile = lax.fori_loop(
        0, devices, lambda n, acc: acc + stat_in[n], jnp.zeros((8, LANES), F32)
    )

    def column_of(first):
        return jnp.concatenate(
            [
                jnp.broadcast_to(tile[:, first + g : first + g + 1], (8, LANES))
                for g in range(groups)
            ],
            axis=0,
        )

    exp_total = column_of(0)
    loss_ref[...] = jnp.log(exp_total) - column_of(groups)
    score_grad = (
        (powers / wide(exp_total) - jnp.where(mask, 1.0, 0.0)) * (1.0 - squash * squash)
    ).astype(BF16)
    sg_ref[...] = score_grad
    scatter(score_grad, GRAD, grad_out, grad_in)

    def backward():
        take(grad_in, recv_sem.at[GRAD])
        grad = spread_rows(total(grad_in)) * spread_rows(fgain_ref[...].astype(F32))

        def back(normed, scale, grad):
            mean = jnp.sum(grad * normed, axis=1, keepdims=True) * (1.0 / dim)
            return scale * (grad - normed * mean)

        dy = rounded(back(*norm(layer_in[layers]), grad))

        def layer(step, dy):
            index = layers - 1 - step
            gain, first, second = weights(index)
            normed, scale = norm(layer_in[index])
            pre = jnp.sum(rounded(normed * gain) * first, axis=1, keepdims=True)
            hidden_grad = jnp.sum(dy * second, axis=1, keepdims=True)
            pre_grad = rounded(hidden_grad * gelu_slope(pre))
            act_grad = jnp.sum(pre_grad * first, axis=0, keepdims=True)
            return rounded(dy + back(normed, scale, act_grad * gain))

        pack_row(lax.fori_loop(0, layers, layer, dy), emb_out)

    if_own(backward)
    gather(EMB, emb_out, emb_in)
    take(emb_in, recv_sem.at[EMB])
    unpack(emb_in, emb_ref)

    take(idbuf.at[pl.ds(0, replicas - 1)], send_sem.at[IDS])
    for phase, buf in ((GAIN, gains), (WIN, wins), (WOUT, wouts)):
        take(buf.at[pl.ds(0, sections - 1)], send_sem.at[phase])
    take(stat_in.at[pl.ds(0, devices - 1)], send_sem.at[STAT])

    def owned():
        take(look_out.at[pl.ds(0, tokens - 1)], send_sem.at[LOOK])
        take(grad_out.at[pl.ds(0, tokens - 1)], send_sem.at[GRAD])
        take(look_in.at[pl.ds(0, devices - 1)], send_sem.at[HEAD])
        take(grad_in.at[pl.ds(0, devices - 1)], send_sem.at[EMB])

    if_own(owned)
    if not all_own:

        @pl.when(jnp.logical_not(own))
        def _():
            take(look_out, send_sem.at[LOOK])
            take(grad_out, send_sem.at[GRAD])


def table_kernel(scale, sg_ref, chosen_ref, head_ref, emb_ref, out_ref):
    over = (((0,), (0,)), ((), ()))
    head = lax.dot_general(sg_ref[...], head_ref[...], over, preferred_element_type=F32)
    emb = lax.dot_general(chosen_ref[...], emb_ref[...], over, preferred_element_type=F32)
    out_ref[...] = (head + emb * scale).astype(BF16)


def per_device(token_ids, target_ids, table, norm_gain, w_in, w_out, final_gain):
    sections, replicas = lax.axis_size("section"), lax.axis_size("dp")
    batches, width = token_ids.shape
    rows_dev, dim = table.shape
    rank = w_in.shape[2]
    per_dp = batches * width
    tokens = replicas * per_dp
    devices = sections * replicas
    chunks = dim // LANES
    pad = (chunks + 15) // 16 * 16
    assert per_dp <= sections and tokens % 8 == 0
    assert chunks % 2 == 0 and rows_dev % LANES == 0
    ids = jnp.concatenate([token_ids.reshape(per_dp), target_ids.reshape(per_dp)])
    ids = jnp.broadcast_to(ids[:, None], (2 * per_dp, LANES))
    fill = lambda rows: jnp.pad(
        rows.reshape(rows.shape[:-1] + (chunks, LANES)),
        ((0, 0),) * (rows.ndim - 1) + ((0, pad - chunks), (0, 0)),
    )
    block = (pad, LANES)
    vmem = pl.BlockSpec(memory_space=pltpu.VMEM)
    loss, score_grad, chosen, head, emb = pl.pallas_call(
        functools.partial(cascade, sections, replicas, per_dp, pad),
        out_shape=(
            jax.ShapeDtypeStruct((tokens, LANES), F32),
            jax.ShapeDtypeStruct((tokens, rows_dev), BF16),
            jax.ShapeDtypeStruct((tokens, rows_dev), BF16),
            jax.ShapeDtypeStruct((tokens, dim), BF16),
            jax.ShapeDtypeStruct((tokens, dim), BF16),
        ),
        in_specs=[vmem] * 6,
        out_specs=(vmem,) * 5,
        scratch_shapes=[
            pltpu.VMEM((replicas, 2 * per_dp, LANES), jnp.int32),
            pltpu.VMEM((2, tokens, LANES), jnp.int32),
            pltpu.VMEM((sections, 2) + block, BF16),
            pltpu.VMEM((sections, 2, rank, dim), BF16),
            pltpu.VMEM((sections, 2, rank, dim), BF16),
            pltpu.VMEM((tokens * pad, LANES), F32),
            pltpu.VMEM((tokens,) + block, BF16),
            pltpu.VMEM((devices,) + block, BF16),
            pltpu.VMEM(block, F32),
            pltpu.VMEM((2 * sections + 1, 8, dim), F32),
            pltpu.VMEM(block, BF16),
            pltpu.VMEM((tokens,) + block, BF16),
            pltpu.VMEM((8, LANES), F32),
            pltpu.VMEM((devices, 8, LANES), F32),
            pltpu.VMEM((tokens,) + block, BF16),
            pltpu.VMEM((devices,) + block, BF16),
            pltpu.VMEM(block, BF16),
            pltpu.VMEM((tokens,) + block, BF16),
            pltpu.SemaphoreType.DMA((9,)),
            pltpu.SemaphoreType.DMA((9,)),
        ],
        compiler_params=pltpu.CompilerParams(
            collective_id=0, has_side_effects=True, vmem_limit_bytes=52 << 20
        ),
        name="cascade",
    )(ids, table, fill(norm_gain[:, 0]), w_in[:, 0], w_out[:, 0], fill(final_gain))
    step = 512
    full = pl.BlockSpec((tokens, rows_dev), lambda i: (0, 0))
    piece = pl.BlockSpec((tokens, step), lambda i: (0, i))
    table_grad = pl.pallas_call(
        functools.partial(table_kernel, math.sqrt(dim)),
        out_shape=jax.ShapeDtypeStruct((rows_dev, dim), BF16),
        grid=(dim // step,),
        in_specs=[full, full, piece, piece],
        out_specs=pl.BlockSpec((rows_dev, step), lambda i: (0, i)),
        name="table_grad",
    )(score_grad, chosen, head, emb)
    token_loss = lax.dynamic_slice_in_dim(
        loss[:, 0], lax.axis_index("dp") * per_dp, per_dp, 0
    ).reshape(batches, width)
    return (token_loss, table_grad)


def solution(mesh):
    return jax.shard_map(
        per_device,
        mesh=mesh,
        in_specs=(
            P(None, "dp"),
            P(None, "dp"),
            P(("section", "dp"), None),
            P(None, "section", None),
            P(None, "section", None, None),
            P(None, "section", None, None),
            P(),
        ),
        out_specs=(P(None, "dp"), P(("section", "dp"), None)),
        check_vma=False,
    )
```

```python
import functools
import math

import jax
import jax.numpy as jnp
from jax import lax
from jax.experimental import pallas as pl
from jax.experimental.pallas import tpu as pltpu
from jax.sharding import PartitionSpec as P

EPS = 1e-06
CAP = 30.0
GELU_C = 0.7978845608028654
LANES = 128
F32 = jnp.float32
BF16 = jnp.bfloat16
IDS, LOOK, HEAD, STAT, GRAD, EMB, GAIN, WIN, WOUT = range(9)
RELAY = 3
TABLE = 12


def gelu_tanh(values):
    return 0.5 * values * (1.0 + jnp.tanh(GELU_C * (values + 0.044715 * values * values * values)))


def gelu_slope(values):
    inner = jnp.tanh(GELU_C * (values + 0.044715 * values * values * values))
    return 0.5 * (1.0 + inner) + 0.5 * values * (1.0 - inner * inner) * GELU_C * (
        1.0 + 3.0 * 0.044715 * values * values
    )


def rounded(values):
    return values.astype(BF16).astype(F32)


def cascade(
    sections, replicas, per_dp, pad,
    ids_ref, table_hbm, gain_ref, win_ref, wout_ref,
    loss_ref, left_ref, right_ref,
    idbuf, idrow, gains, wins, wouts, flat, look_out, look_in, tok, layer_in,
    head_out, head_in, stat_out, stat_in, grad_out, grad_in, emb_out, emb_in,
    table_ref, gain_wide, kept, send_sem, recv_sem,
):
    devices = sections * replicas
    tokens = replicas * per_dp
    rows_dev, dim = table_ref.shape
    chunks = dim // LANES
    head_ref = right_ref.at[pl.ds(0, tokens)]
    layers = 2 * sections
    scale_in = math.sqrt(dim)
    sec, rep = lax.axis_index("section"), lax.axis_index("dp")
    me = sec * replicas + rep
    offset = me * rows_dev
    all_own = per_dp == sections
    own = sec < per_dp
    my_token = rep * per_dp + sec if all_own else jnp.where(own, rep * per_dp + sec, -1)

    def if_own(body):
        if all_own:
            body()
        else:
            pl.when(own)(body)

    def spread(phase, count, first, target, skip, src, dst):
        def step(i, _):
            at = lax.rem(first + i, count)

            @pl.when(at != skip)
            def _():
                pltpu.make_async_remote_copy(
                    src_ref=src(at),
                    dst_ref=dst,
                    send_sem=send_sem.at[phase],
                    recv_sem=recv_sem.at[phase],
                    device_id=target(at),
                    device_id_type=pl.DeviceIdType.MESH,
                ).start()

            @pl.when(at == skip)
            def _():
                pltpu.make_async_copy(src(at), dst, recv_sem.at[phase]).start()

            return 0

        lax.fori_loop(0, count, step, 0, unroll=4)

    def take(ref, sem):
        pltpu.make_async_copy(ref, ref, sem).wait()

    def any_device(n):
        return (n // replicas, n % replicas)

    def token_device(t):
        return (t % per_dp, t // per_dp)

    load = pltpu.make_async_copy(table_hbm, table_ref, recv_sem.at[TABLE])
    load.start()
    barrier = pltpu.get_barrier_semaphore()

    def greet(i, _):
        n = lax.rem(me + 1 + i, devices)
        pl.semaphore_signal(
            barrier, inc=1, device_id=any_device(n), device_id_type=pl.DeviceIdType.MESH
        )
        return 0

    lax.fori_loop(0, devices - 1, greet, 0)
    flat[...] = jnp.zeros_like(flat)
    tok[...] = jnp.zeros_like(tok)
    pl.semaphore_wait(barrier, devices - 1)

    spread(IDS, replicas, rep, lambda d: (sec, d), rep, lambda d: ids_ref, idbuf.at[rep])
    half = sections // 2
    side, partner = sec % 2, sec + 1 - 2 * (sec % 2)
    stores = ((GAIN, gain_ref, gains), (WIN, win_ref, wins), (WOUT, wout_ref, wouts))
    for phase, src, dst in stores:
        for i in range(1, half):
            pair = lax.rem(sec // 2 + i, half)
            pltpu.make_async_remote_copy(
                src_ref=src,
                dst_ref=dst.at[side, sec // 2],
                send_sem=send_sem.at[phase],
                recv_sem=recv_sem.at[phase],
                device_id=(2 * pair + side, rep),
                device_id_type=pl.DeviceIdType.MESH,
            ).start()
        pltpu.make_async_copy(src, dst.at[side, sec // 2], recv_sem.at[phase]).start()

    take(idbuf, recv_sem.at[IDS])
    for d in range(replicas):
        for kind in range(2):
            for k in range(per_dp):
                idrow[kind, pl.ds(d * per_dp + k, 1), :] = idbuf[
                    d, pl.ds(kind * per_dp + k, 1), :
                ]
    wide = lambda value: jnp.concatenate([value] * (rows_dev // LANES), axis=1)
    column = lax.broadcasted_iota(jnp.int32, (tokens, rows_dev), 1) + offset
    chosen = jnp.where(wide(idrow[0]) == column, 1.0, 0.0).astype(BF16)
    mask = wide(idrow[1]) == column
    left_ref[pl.ds(tokens, tokens), :] = chosen
    left_ref[pl.ds(2 * tokens, tokens), :] = chosen
    load.wait()

    def scatter(left, phase, out, into):
        for j in range(0, chunks, 2):
            part = jnp.dot(
                left, table_ref[:, j * LANES : (j + 2) * LANES], preferred_element_type=F32
            )
            flat[pl.ds(j, tokens, stride=pad), :] = part[:, :LANES]
            flat[pl.ds(j + 1, tokens, stride=pad), :] = part[:, LANES:]
        out[...] = flat[...].reshape(tokens, pad // 8, 8, LANES).astype(BF16)
        spread(
            phase, tokens, rep * per_dp + sec, token_device, my_token,
            lambda t: out.at[t], into.at[me],
        )

    def total(into):
        return lax.fori_loop(
            0, devices, lambda n, acc: acc + into[n].astype(F32),
            jnp.zeros((pad // 8, 8, LANES), F32),
            unroll=4,
        ).reshape(pad, LANES)

    def spread_rows(values):
        tok[...] = values
        return jnp.concatenate(
            [jnp.broadcast_to(tok[j : j + 1, :], (8, LANES)) for j in range(chunks)], axis=1
        )

    def pack_row(values, out):
        for j in range(chunks):
            tok[j : j + 1, :] = values[0:1, j * LANES : (j + 1) * LANES]
        out[...] = tok[...].reshape(pad // 8, 8, LANES).astype(BF16)

    def norm(x):
        scale = lax.rsqrt(jnp.sum(x * x, axis=1, keepdims=True) * (1.0 / dim) + EPS)
        return x * scale, scale

    def weights(layer):
        s, c = layer % sections, layer // sections
        at = (s % 2, s // 2, c, 0)
        return gain_wide[layer], wins[at].astype(F32), wouts[at].astype(F32)

    def widen(layer, _):
        s, c = layer % sections, layer // sections
        gain_wide[layer] = spread_rows(gains[s % 2, s // 2, c].astype(F32).reshape(pad, LANES))
        return 0

    def gather(phase, block, into):
        if_own(
            lambda: spread(
                phase, devices, me, any_device, me, lambda n: block, into.at[my_token]
            )
        )

    def unpack(into, out):
        flat[...] = into[...].astype(F32).reshape(tokens * pad, LANES)
        for j in range(chunks):
            out(slice(j * LANES, (j + 1) * LANES), flat[pl.ds(j, tokens, stride=pad), :])

    scatter(chosen, LOOK, look_out, look_in)
    for phase, _, buf in stores:
        take(buf.at[side], recv_sem.at[phase])
        pltpu.make_async_remote_copy(
            src_ref=buf.at[side],
            dst_ref=buf.at[side],
            send_sem=send_sem.at[phase + RELAY],
            recv_sem=recv_sem.at[phase + RELAY],
            device_id=(partner, rep),
            device_id_type=pl.DeviceIdType.MESH,
        ).start()
    gain_wide[layers] = spread_rows(gain_ref[2].astype(F32).reshape(pad, LANES))
    take(gains.at[1 - side], recv_sem.at[GAIN + RELAY])
    lax.fori_loop(0, layers, widen, 0)
    for phase, _, buf in stores[1:]:
        take(buf.at[1 - side], recv_sem.at[phase + RELAY])

    def forward():
        take(look_in, recv_sem.at[LOOK])
        x = spread_rows(rounded(total(look_in) * scale_in))

        def layer(index, x):
            layer_in[index] = x
            gain, first, second = weights(index)
            normed, scale = norm(x)
            pre = jnp.sum(rounded(normed * gain) * first, axis=1, keepdims=True)
            hidden = rounded(gelu_tanh(pre))
            kept[index, 0] = jnp.broadcast_to(scale, (8, LANES))
            kept[index, 1] = jnp.broadcast_to(gelu_slope(pre), (8, LANES))
            return rounded(x + jnp.sum(hidden * second, axis=0, keepdims=True))

        x = lax.fori_loop(0, layers, layer, x)
        layer_in[layers] = x
        normed, _ = norm(x)
        pack_row(normed * gain_wide[layers], head_out)

    if_own(forward)
    gather(HEAD, head_out, head_in)
    take(head_in, recv_sem.at[HEAD])

    def store_head(lanes, part):
        right_ref[pl.ds(0, tokens), lanes] = part.astype(BF16)

    unpack(head_in, store_head)

    scores = lax.dot_general(
        head_ref[...], table_ref[...], (((1,), (1,)), ((), ())), preferred_element_type=F32
    )
    squash = jnp.tanh(scores / CAP)
    capped = CAP * squash
    powers = jnp.exp(capped)
    exp_sum = jnp.sum(powers, axis=1, keepdims=True)
    goal = jnp.sum(jnp.where(mask, capped, 0.0), axis=1, keepdims=True)
    groups = tokens // 8
    lane = lax.broadcasted_iota(jnp.int32, (8, LANES), 1)
    tile = jnp.zeros((8, LANES), F32)
    for g in range(groups):
        tile = jnp.where(lane == g, exp_sum[8 * g : 8 * g + 8], tile)
        tile = jnp.where(lane == groups + g, goal[8 * g : 8 * g + 8], tile)
    stat_out[...] = tile
    spread(STAT, devices, me, any_device, me, lambda n: stat_out, stat_in.at[me])
    take(stat_in, recv_sem.at[STAT])
    tile = lax.fori_loop(
        0, devices, lambda n, acc: acc + stat_in[n], jnp.zeros((8, LANES), F32)
    )

    def column_of(first):
        return jnp.concatenate(
            [
                jnp.broadcast_to(tile[:, first + g : first + g + 1], (8, LANES))
                for g in range(groups)
            ],
            axis=0,
        )

    exp_total = column_of(0)
    loss_ref[...] = jnp.log(exp_total) - column_of(groups)
    score_grad = (
        (powers / wide(exp_total) - jnp.where(mask, 1.0, 0.0)) * (1.0 - squash * squash)
    ).astype(BF16)
    left_ref[pl.ds(0, tokens), :] = score_grad
    scatter(score_grad, GRAD, grad_out, grad_in)

    def backward():
        take(grad_in, recv_sem.at[GRAD])
        grad = spread_rows(total(grad_in)) * gain_wide[layers]

        def back(normed, scale, grad):
            mean = jnp.sum(grad * normed, axis=1, keepdims=True) * (1.0 / dim)
            return scale * (grad - normed * mean)

        dy = rounded(back(*norm(layer_in[layers]), grad))

        def layer(step, dy):
            index = layers - 1 - step
            gain, first, second = weights(index)
            scale = kept[index, 0][:, 0:1]
            normed = layer_in[index] * scale
            hidden_grad = jnp.sum(dy * second, axis=1, keepdims=True)
            pre_grad = rounded(hidden_grad * kept[index, 1][:, 0:1])
            act_grad = jnp.sum(pre_grad * first, axis=0, keepdims=True)
            return rounded(dy + back(normed, scale, act_grad * gain))

        pack_row(lax.fori_loop(0, layers, layer, dy), emb_out)

    if_own(backward)
    gather(EMB, emb_out, emb_in)
    take(emb_in, recv_sem.at[EMB])

    def store_emb(lanes, part):
        part = part * scale_in
        high = part.astype(BF16)
        right_ref[pl.ds(tokens, tokens), lanes] = high
        right_ref[pl.ds(2 * tokens, tokens), lanes] = (part - high.astype(F32)).astype(BF16)

    unpack(emb_in, store_emb)

    take(idbuf.at[pl.ds(0, replicas - 1)], send_sem.at[IDS])
    for phase, _, buf in stores:
        if half > 1:
            take(buf.at[0, pl.ds(0, half - 1)], send_sem.at[phase])
        take(buf.at[0], send_sem.at[phase + RELAY])
    take(stat_in.at[pl.ds(0, devices - 1)], send_sem.at[STAT])

    def owned():
        take(look_out.at[pl.ds(0, tokens - 1)], send_sem.at[LOOK])
        take(grad_out.at[pl.ds(0, tokens - 1)], send_sem.at[GRAD])
        take(look_in.at[pl.ds(0, devices - 1)], send_sem.at[HEAD])
        take(grad_in.at[pl.ds(0, devices - 1)], send_sem.at[EMB])

    if_own(owned)
    if not all_own:

        @pl.when(jnp.logical_not(own))
        def _():
            take(look_out, send_sem.at[LOOK])
            take(grad_out, send_sem.at[GRAD])


def table_kernel(left_ref, right_ref, out_ref):
    over = (((0,), (0,)), ((), ()))
    out_ref[...] = lax.dot_general(
        left_ref[...], right_ref[...], over, preferred_element_type=F32
    ).astype(BF16)


def per_device(token_ids, target_ids, table, norm_gain, w_in, w_out, final_gain):
    sections, replicas = lax.axis_size("section"), lax.axis_size("dp")
    batches, width = token_ids.shape
    rows_dev, dim = table.shape
    rank = w_in.shape[2]
    per_dp = batches * width
    tokens = replicas * per_dp
    devices = sections * replicas
    chunks = dim // LANES
    pad = (chunks + 7) // 8 * 8
    assert per_dp <= sections and tokens % 8 == 0
    assert chunks % 2 == 0 and rows_dev % LANES == 0
    ids = jnp.concatenate([token_ids.reshape(per_dp), target_ids.reshape(per_dp)])
    ids = jnp.broadcast_to(ids[:, None], (2 * per_dp, LANES))
    gain_rows = jnp.concatenate([norm_gain[:, 0], final_gain[None]])
    gain_rows = jnp.pad(gain_rows, ((0, 0), (0, pad * LANES - dim))).reshape(
        3, pad // 8, 8, LANES
    )
    block = (pad // 8, 8, LANES)
    vmem = pl.BlockSpec(memory_space=pltpu.VMEM)
    anywhere = pl.BlockSpec(memory_space=pl.ANY)
    loss, left, right = pl.pallas_call(
        functools.partial(cascade, sections, replicas, per_dp, pad),
        out_shape=(
            jax.ShapeDtypeStruct((tokens, LANES), F32),
            jax.ShapeDtypeStruct((3 * tokens, rows_dev), BF16),
            jax.ShapeDtypeStruct((3 * tokens, dim), BF16),
        ),
        in_specs=[vmem, anywhere, vmem, anywhere, anywhere],
        out_specs=(vmem,) * 3,
        scratch_shapes=[
            pltpu.VMEM((replicas, 2 * per_dp, LANES), jnp.int32),
            pltpu.VMEM((2, tokens, LANES), jnp.int32),
            pltpu.VMEM((2, sections // 2, 3) + block, BF16),
            pltpu.VMEM((2, sections // 2, 2, 1, rank, dim), BF16),
            pltpu.VMEM((2, sections // 2, 2, 1, rank, dim), BF16),
            pltpu.VMEM((tokens * pad, LANES), F32),
            pltpu.VMEM((tokens,) + block, BF16),
            pltpu.VMEM((devices,) + block, BF16),
            pltpu.VMEM((pad, LANES), F32),
            pltpu.VMEM((2 * sections + 1, 8, dim), F32),
            pltpu.VMEM(block, BF16),
            pltpu.VMEM((tokens,) + block, BF16),
            pltpu.VMEM((8, LANES), F32),
            pltpu.VMEM((devices, 8, LANES), F32),
            pltpu.VMEM((tokens,) + block, BF16),
            pltpu.VMEM((devices,) + block, BF16),
            pltpu.VMEM(block, BF16),
            pltpu.VMEM((tokens,) + block, BF16),
            pltpu.VMEM((rows_dev, dim), BF16),
            pltpu.VMEM((2 * sections + 1, 8, dim), F32),
            pltpu.VMEM((2 * sections, 2, 8, LANES), F32),
            pltpu.SemaphoreType.DMA((13,)),
            pltpu.SemaphoreType.DMA((13,)),
        ],
        compiler_params=pltpu.CompilerParams(
            collective_id=0, has_side_effects=True, vmem_limit_bytes=52 << 20
        ),
        name="cascade",
    )(ids, table, gain_rows, w_in, w_out)
    step = dim // 3
    table_grad = pl.pallas_call(
        table_kernel,
        out_shape=jax.ShapeDtypeStruct((rows_dev, dim), BF16),
        grid=(dim // step,),
        in_specs=[
            pl.BlockSpec((3 * tokens, rows_dev), lambda i: (0, 0)),
            pl.BlockSpec((3 * tokens, step), lambda i: (0, i)),
        ],
        out_specs=pl.BlockSpec((rows_dev, step), lambda i: (0, i)),
        name="table_grad",
    )(left, right)
    token_loss = lax.dynamic_slice_in_dim(
        loss[:, 0], lax.axis_index("dp") * per_dp, per_dp, 0
    ).reshape(batches, width)
    return (token_loss, table_grad)


def solution(mesh):
    return jax.shard_map(
        per_device,
        mesh=mesh,
        in_specs=(
            P(None, "dp"),
            P(None, "dp"),
            P(("section", "dp"), None),
            P(None, "section", None),
            P(None, "section", None, None),
            P(None, "section", None, None),
            P(),
        ),
        out_specs=(P(None, "dp"), P(("section", "dp"), None)),
        check_vma=False,
    )
```

```python
import functools
import math

import jax
import jax.numpy as jnp
from jax import lax
from jax.experimental import pallas as pl
from jax.experimental.pallas import tpu as pltpu
from jax.sharding import PartitionSpec as P

EPS = 1e-06
CAP = 30.0
GELU_C = 0.7978845608028654
LANES = 128
F32 = jnp.float32
BF16 = jnp.bfloat16
IDS, LOOK, HEAD, STAT, GRAD, EMB, GAIN, WIN, WOUT = range(9)
RELAY = 3
TABLE = 12
PAIR = 13


def gelu_tanh(values):
    return 0.5 * values * (1.0 + jnp.tanh(GELU_C * (values + 0.044715 * values * values * values)))


def gelu_slope(values):
    inner = jnp.tanh(GELU_C * (values + 0.044715 * values * values * values))
    return 0.5 * (1.0 + inner) + 0.5 * values * (1.0 - inner * inner) * GELU_C * (
        1.0 + 3.0 * 0.044715 * values * values
    )


def rounded(values):
    return values.astype(BF16).astype(F32)


def cascade(
    sections, replicas, per_dp, pad,
    token_ref, target_ref, table_hbm, gain_ref, fgain_ref, win_ref, wout_ref,
    loss_ref, left_ref, right_ref,
    loss_all, ids_ref, idbuf, idrow, gains, wins, wouts, flat, look_out, look_in, tok, layer_in,
    head_out, head_in, stat_out, stat_in, grad_out, grad_in, emb_out, emb_in,
    table_ref, gain_wide, kept, look_pair, grad_pair, send_sem, recv_sem,
):
    devices = sections * replicas
    tokens = replicas * per_dp
    rows_dev, dim = table_ref.shape
    chunks = dim // LANES
    head_ref = right_ref.at[pl.ds(0, tokens)]
    layers = 2 * sections
    scale_in = math.sqrt(dim)
    sec, rep = lax.axis_index("section"), lax.axis_index("dp")
    me = sec * replicas + rep
    offset = me * rows_dev
    all_own = per_dp == sections
    own = sec < per_dp
    own_half = per_dp // 2
    count_half = tokens // 2
    half = sections // 2
    side, partner = sec % 2, sec + 1 - 2 * (sec % 2)
    my_half = rep * own_half + sec // 2
    if not all_own:
        my_half = jnp.where(own, my_half, -1)

    def if_own(body):
        if all_own:
            body()
        else:
            pl.when(own)(body)

    def spread(phase, count, first, target, skip, src, dst):
        def step(i, _):
            at = lax.rem(first + i, count)

            @pl.when(at != skip)
            def _():
                pltpu.make_async_remote_copy(
                    src_ref=src(at),
                    dst_ref=dst,
                    send_sem=send_sem.at[phase],
                    recv_sem=recv_sem.at[phase],
                    device_id=target(at),
                    device_id_type=pl.DeviceIdType.MESH,
                ).start()

            @pl.when(at == skip)
            def _():
                pltpu.make_async_copy(src(at), dst, recv_sem.at[phase]).start()

            return 0

        lax.fori_loop(0, count, step, 0, unroll=8)

    def take(ref, sem):
        pltpu.make_async_copy(ref, ref, sem).wait()

    def any_device(n):
        return (n // replicas, n % replicas)

    def token_device(h):
        return (2 * (h % own_half) + side, h // own_half)

    def side_device(q):
        return (2 * (q // replicas) + side, q % replicas)

    side_me = (sec // 2) * replicas + rep

    def pair_copy(phase, src, dst):
        return pltpu.make_async_remote_copy(
            src_ref=src,
            dst_ref=dst,
            send_sem=send_sem.at[phase],
            recv_sem=recv_sem.at[phase],
            device_id=(partner, rep),
            device_id_type=pl.DeviceIdType.MESH,
        )

    load = pltpu.make_async_copy(table_hbm, table_ref, recv_sem.at[TABLE])
    load.start()
    barrier = pltpu.get_barrier_semaphore()

    def greet(i, _):
        n = lax.rem(me + 1 + i, devices)
        pl.semaphore_signal(
            barrier, inc=1, device_id=any_device(n), device_id_type=pl.DeviceIdType.MESH
        )
        return 0

    lax.fori_loop(0, devices - 1, greet, 0, unroll=8)
    flat[...] = jnp.zeros_like(flat)
    tok[...] = jnp.zeros_like(tok)
    row = lax.broadcasted_iota(jnp.int32, (2 * per_dp, LANES), 0)
    made = jnp.zeros((2 * per_dp, LANES), jnp.int32)
    batches, width = token_ref.shape
    for b in range(batches):
        for w in range(width):
            k = b * width + w
            made = jnp.where(row == k, token_ref[b : b + 1, w : w + 1], made)
            made = jnp.where(row == per_dp + k, target_ref[b : b + 1, w : w + 1], made)
    ids_ref[...] = made
    pl.semaphore_wait(barrier, devices - 1)

    spread(IDS, replicas, rep, lambda d: (sec, d), rep, lambda d: ids_ref, idbuf.at[rep])
    stores = ((GAIN, gain_ref, gains), (WIN, win_ref, wins), (WOUT, wout_ref, wouts))
    for phase, src, dst in stores:
        for i in range(1, half):
            pair = lax.rem(sec // 2 + i, half)
            pltpu.make_async_remote_copy(
                src_ref=src,
                dst_ref=dst.at[side, sec // 2],
                send_sem=send_sem.at[phase],
                recv_sem=recv_sem.at[phase],
                device_id=(2 * pair + side, rep),
                device_id_type=pl.DeviceIdType.MESH,
            ).start()
        pltpu.make_async_copy(src, dst.at[side, sec // 2], recv_sem.at[phase]).start()

    take(idbuf, recv_sem.at[IDS])
    for d in range(replicas):
        for kind in range(2):
            for k in range(per_dp):
                at = (k % 2) * count_half + d * own_half + k // 2
                idrow[kind, pl.ds(at, 1), :] = idbuf[
                    d, pl.ds(kind * per_dp + k, 1), :
                ]
    wide = lambda value: jnp.concatenate([value] * (rows_dev // LANES), axis=1)
    column = lax.broadcasted_iota(jnp.int32, (tokens, rows_dev), 1) + offset
    chosen = jnp.where(wide(idrow[0]) == column, 1.0, 0.0).astype(BF16)
    mask = wide(idrow[1]) == column
    left_ref[pl.ds(tokens, tokens), :] = chosen
    left_ref[pl.ds(2 * tokens, tokens), :] = chosen
    load.wait()

    def scatter(left, phase, out, pair, into):
        for j in range(0, chunks, 2):
            part = jnp.dot(
                left, table_ref[:, j * LANES : (j + 2) * LANES], preferred_element_type=F32
            )
            flat[pl.ds(j, tokens, stride=pad), :] = part[:, :LANES]
            flat[pl.ds(j + 1, tokens, stride=pad), :] = part[:, LANES:]
        mine = pl.ds(pl.multiple_of(side * (count_half * pad), 8), count_half * pad)
        away = pl.ds(pl.multiple_of((1 - side) * (count_half * pad), 8), count_half * pad)
        blocks = (count_half, pad // 8, 8, LANES)
        out[1 - side] = flat[away, :].reshape(blocks).astype(BF16)
        swap = pair_copy(phase + PAIR, out.at[1 - side], pair)
        swap.start()
        swap.wait()
        out[side] = (flat[mine, :].reshape(blocks) + pair[...].astype(F32)).astype(BF16)
        spread(
            phase, count_half, rep * own_half + sec // 2, token_device, my_half,
            lambda h: out.at[side, h], into.at[side_me],
        )

    def total(into):
        return lax.fori_loop(
            0, devices // 2, lambda n, acc: acc + into[n].astype(F32),
            jnp.zeros((pad // 8, 8, LANES), F32),
            unroll=4,
        ).reshape(pad, LANES)

    def spread_rows(values):
        tok[...] = values
        return jnp.concatenate(
            [jnp.broadcast_to(tok[j : j + 1, :], (8, LANES)) for j in range(chunks)], axis=1
        )

    def pack_row(values, out):
        for j in range(chunks):
            tok[j : j + 1, :] = values[0:1, j * LANES : (j + 1) * LANES]
        out[...] = tok[...].reshape(pad // 8, 8, LANES).astype(BF16)

    def norm(x):
        scale = lax.rsqrt(jnp.sum(x * x, axis=1, keepdims=True) * (1.0 / dim) + EPS)
        return x * scale, scale

    def weights(layer):
        s, c = layer % sections, layer // sections
        at = (s % 2, s // 2, c, 0)
        return gain_wide[layer], wins[at].astype(F32), wouts[at].astype(F32)

    def widen(layer, _):
        s, c = layer % sections, layer // sections
        both = gains[s % 2, s // 2].astype(F32)
        picked = jnp.where(c == 0, both[0:1], both[1:2])
        gain_wide[layer] = jnp.broadcast_to(picked, (8, dim))
        return 0

    def gather(phase, block, into):
        if_own(
            lambda: spread(
                phase, devices // 2, side_me, side_device, side_me,
                lambda n: block, into.at[side, my_half],
            )
        )
        take(into.at[side], recv_sem.at[phase])
        relay = pair_copy(phase + PAIR, into.at[side], into.at[side])
        relay.start()
        relay.wait()

    def unpack(into, out):
        flat[...] = into[...].astype(F32).reshape(tokens * pad, LANES)
        for j in range(chunks):
            out(slice(j * LANES, (j + 1) * LANES), flat[pl.ds(j, tokens, stride=pad), :])

    scatter(chosen, LOOK, look_out, look_pair, look_in)
    for phase, _, buf in stores:
        take(buf.at[side], recv_sem.at[phase])
        pltpu.make_async_remote_copy(
            src_ref=buf.at[side],
            dst_ref=buf.at[side],
            send_sem=send_sem.at[phase + RELAY],
            recv_sem=recv_sem.at[phase + RELAY],
            device_id=(partner, rep),
            device_id_type=pl.DeviceIdType.MESH,
        ).start()
    gain_wide[layers] = jnp.broadcast_to(fgain_ref[...].astype(F32), (8, dim))
    take(gains.at[1 - side], recv_sem.at[GAIN + RELAY])
    lax.fori_loop(0, layers, widen, 0)
    for phase, _, buf in stores[1:]:
        take(buf.at[1 - side], recv_sem.at[phase + RELAY])

    def forward():
        take(look_in, recv_sem.at[LOOK])
        x = spread_rows(rounded(total(look_in) * scale_in))

        def layer(index, x):
            layer_in[index] = x
            gain, first, second = weights(index)
            normed, scale = norm(x)
            pre = jnp.sum(rounded(normed * gain) * first, axis=1, keepdims=True)
            hidden = rounded(gelu_tanh(pre))
            kept[index, 0] = jnp.broadcast_to(scale, (8, LANES))
            kept[index, 1] = jnp.broadcast_to(gelu_slope(pre), (8, LANES))
            return rounded(x + jnp.sum(hidden * second, axis=0, keepdims=True))

        x = lax.fori_loop(0, layers, layer, x)
        layer_in[layers] = x
        normed, _ = norm(x)
        pack_row(normed * gain_wide[layers], head_out)

    if_own(forward)
    gather(HEAD, head_out, head_in)

    def store_head(lanes, part):
        right_ref[pl.ds(0, tokens), lanes] = part.astype(BF16)

    unpack(head_in, store_head)

    scores = lax.dot_general(
        head_ref[...], table_ref[...], (((1,), (1,)), ((), ())), preferred_element_type=F32
    )
    squash = jnp.tanh(scores / CAP)
    capped = CAP * squash
    powers = jnp.exp(capped)
    exp_sum = jnp.sum(powers, axis=1, keepdims=True)
    goal = jnp.sum(jnp.where(mask, capped, 0.0), axis=1, keepdims=True)
    groups = tokens // 8
    lane = lax.broadcasted_iota(jnp.int32, (8, LANES), 1)
    tile = jnp.zeros((8, LANES), F32)
    for g in range(groups):
        tile = jnp.where(lane == g, exp_sum[8 * g : 8 * g + 8], tile)
        tile = jnp.where(lane == groups + g, goal[8 * g : 8 * g + 8], tile)
    stat_out[...] = tile
    spread(STAT, devices, me, any_device, me, lambda n: stat_out, stat_in.at[me])
    take(stat_in, recv_sem.at[STAT])
    tile = lax.fori_loop(
        0, devices, lambda n, acc: acc + stat_in[n], jnp.zeros((8, LANES), F32)
    )

    def column_of(first):
        return jnp.concatenate(
            [
                jnp.broadcast_to(tile[:, first + g : first + g + 1], (8, LANES))
                for g in range(groups)
            ],
            axis=0,
        )

    exp_total = column_of(0)
    loss_all[...] = jnp.log(exp_total) - column_of(groups)
    for b in range(batches):
        for w in range(width):
            k = b * width + w
            at = (k % 2) * count_half + rep * own_half + k // 2
            loss_ref[b : b + 1, w : w + 1] = loss_all[pl.ds(at, 1), 0:1]
    score_grad = (
        (powers / wide(exp_total) - jnp.where(mask, 1.0, 0.0)) * (1.0 - squash * squash)
    ).astype(BF16)
    left_ref[pl.ds(0, tokens), :] = score_grad
    scatter(score_grad, GRAD, grad_out, grad_pair, grad_in)

    def backward():
        take(grad_in, recv_sem.at[GRAD])
        grad = spread_rows(total(grad_in)) * gain_wide[layers]

        def back(normed, scale, grad):
            mean = jnp.sum(grad * normed, axis=1, keepdims=True) * (1.0 / dim)
            return scale * (grad - normed * mean)

        dy = rounded(back(*norm(layer_in[layers]), grad))

        def layer(step, dy):
            index = layers - 1 - step
            gain, first, second = weights(index)
            scale = kept[index, 0][:, 0:1]
            normed = layer_in[index] * scale
            hidden_grad = jnp.sum(dy * second, axis=1, keepdims=True)
            pre_grad = rounded(hidden_grad * kept[index, 1][:, 0:1])
            act_grad = jnp.sum(pre_grad * first, axis=0, keepdims=True)
            return rounded(dy + back(normed, scale, act_grad * gain))

        pack_row(lax.fori_loop(0, layers, layer, dy), emb_out)

    if_own(backward)
    gather(EMB, emb_out, emb_in)

    def store_emb(lanes, part):
        part = part * scale_in
        high = part.astype(BF16)
        right_ref[pl.ds(tokens, tokens), lanes] = high
        right_ref[pl.ds(2 * tokens, tokens), lanes] = (part - high.astype(F32)).astype(BF16)

    unpack(emb_in, store_emb)

    take(idbuf.at[pl.ds(0, replicas - 1)], send_sem.at[IDS])
    for phase, _, buf in stores:
        if half > 1:
            take(buf.at[0, pl.ds(0, half - 1)], send_sem.at[phase])
        take(buf.at[0], send_sem.at[phase + RELAY])
    take(stat_in.at[pl.ds(0, devices - 1)], send_sem.at[STAT])

    def owned():
        take(look_pair.at[pl.ds(0, count_half - 1)], send_sem.at[LOOK])
        take(grad_pair.at[pl.ds(0, count_half - 1)], send_sem.at[GRAD])
        take(look_in.at[pl.ds(0, devices // 2 - 1)], send_sem.at[HEAD])
        take(grad_in.at[pl.ds(0, devices // 2 - 1)], send_sem.at[EMB])

    if_own(owned)
    if not all_own:

        @pl.when(jnp.logical_not(own))
        def _():
            take(look_pair, send_sem.at[LOOK])
            take(grad_pair, send_sem.at[GRAD])


def table_kernel(left_ref, right_ref, out_ref):
    over = (((0,), (0,)), ((), ()))
    step = out_ref.shape[1]
    lanes = pl.ds(pl.multiple_of(pl.program_id(0) * step, LANES), step)
    out_ref[...] = lax.dot_general(
        left_ref[...], right_ref[:, lanes], over, preferred_element_type=F32
    ).astype(BF16)


def per_device(token_ids, target_ids, table, norm_gain, w_in, w_out, final_gain):
    sections, replicas = lax.axis_size("section"), lax.axis_size("dp")
    batches, width = token_ids.shape
    rows_dev, dim = table.shape
    rank = w_in.shape[2]
    per_dp = batches * width
    tokens = replicas * per_dp
    devices = sections * replicas
    chunks = dim // LANES
    pad = (chunks + 7) // 8 * 8
    assert per_dp <= sections and tokens % 8 == 0
    assert chunks % 2 == 0 and rows_dev % LANES == 0
    assert per_dp % 2 == 0 and sections % 2 == 0
    block = (pad // 8, 8, LANES)
    vmem = pl.BlockSpec(memory_space=pltpu.VMEM)
    hbm = pl.BlockSpec(memory_space=pltpu.HBM)
    token_loss, left, right = pl.pallas_call(
        functools.partial(cascade, sections, replicas, per_dp, pad),
        out_shape=(
            jax.ShapeDtypeStruct((batches, width), F32),
            jax.ShapeDtypeStruct((3 * tokens, rows_dev), BF16),
            jax.ShapeDtypeStruct((3 * tokens, dim), BF16),
        ),
        in_specs=[vmem, vmem, hbm, vmem, vmem, hbm, hbm],
        out_specs=(vmem,) * 3,
        scratch_shapes=[
            pltpu.VMEM((tokens, LANES), F32),
            pltpu.VMEM((2 * per_dp, LANES), jnp.int32),
            pltpu.VMEM((replicas, 2 * per_dp, LANES), jnp.int32),
            pltpu.VMEM((2, tokens, LANES), jnp.int32),
            pltpu.VMEM((2, sections // 2, 2, dim), BF16),
            pltpu.VMEM((2, sections // 2, 2, 1, rank, dim), BF16),
            pltpu.VMEM((2, sections // 2, 2, 1, rank, dim), BF16),
            pltpu.VMEM((tokens * pad, LANES), F32),
            pltpu.VMEM((2, tokens // 2) + block, BF16),
            pltpu.VMEM((devices // 2,) + block, BF16),
            pltpu.VMEM((pad, LANES), F32),
            pltpu.VMEM((2 * sections + 1, 8, dim), F32),
            pltpu.VMEM(block, BF16),
            pltpu.VMEM((2, tokens // 2) + block, BF16),
            pltpu.VMEM((8, LANES), F32),
            pltpu.VMEM((devices, 8, LANES), F32),
            pltpu.VMEM((2, tokens // 2) + block, BF16),
            pltpu.VMEM((devices // 2,) + block, BF16),
            pltpu.VMEM(block, BF16),
            pltpu.VMEM((2, tokens // 2) + block, BF16),
            pltpu.VMEM((rows_dev, dim), BF16),
            pltpu.VMEM((2 * sections + 1, 8, dim), F32),
            pltpu.VMEM((2 * sections, 2, 8, LANES), F32),
            pltpu.VMEM((tokens // 2,) + block, BF16),
            pltpu.VMEM((tokens // 2,) + block, BF16),
            pltpu.SemaphoreType.DMA((19,)),
            pltpu.SemaphoreType.DMA((19,)),
        ],
        compiler_params=pltpu.CompilerParams(
            collective_id=0, has_side_effects=True, vmem_limit_bytes=63400000
        ),
        name="cascade",
    )(token_ids, target_ids, table, norm_gain[:, 0], final_gain[None], w_in, w_out)
    step = dim // 3
    table_grad = pl.pallas_call(
        table_kernel,
        out_shape=jax.ShapeDtypeStruct((rows_dev, dim), BF16),
        grid=(dim // step,),
        in_specs=[vmem, vmem],
        out_specs=pl.BlockSpec((rows_dev, step), lambda i: (0, i)),
        name="table_grad",
    )(left, right)
    return (token_loss, table_grad)


def solution(mesh):
    return jax.shard_map(
        per_device,
        mesh=mesh,
        in_specs=(
            P(None, "dp"),
            P(None, "dp"),
            P(("section", "dp"), None),
            P(None, "section", None),
            P(None, "section", None, None),
            P(None, "section", None, None),
            P(),
        ),
        out_specs=(P(None, "dp"), P(("section", "dp"), None)),
        check_vma=False,
    )
```

```python
import functools
import math

import jax
import jax.numpy as jnp
from jax import lax
from jax.experimental import pallas as pl
from jax.experimental.pallas import tpu as pltpu
from jax.sharding import PartitionSpec as P

EPS = 1e-06
CAP = 30.0
GELU_C = 0.7978845608028654
LANES = 128
F32 = jnp.float32
BF16 = jnp.bfloat16
IDS, LOOK, HEAD, STAT, GRAD, EMB, GAIN, WIN, WOUT = range(9)
RELAY = 3
TABLE = 12
PAIR = 13


def gelu_tanh(values):
    return 0.5 * values * (1.0 + jnp.tanh(GELU_C * (values + 0.044715 * values * values * values)))


def gelu_slope(values):
    inner = jnp.tanh(GELU_C * (values + 0.044715 * values * values * values))
    return 0.5 * (1.0 + inner) + 0.5 * values * (1.0 - inner * inner) * GELU_C * (
        1.0 + 3.0 * 0.044715 * values * values
    )


def rounded(values):
    return values.astype(BF16).astype(F32)


def cascade(
    sections, replicas, per_dp, pad,
    token_ref, target_ref, table_hbm, gain_ref, fgain_ref, win_ref, wout_ref,
    loss_ref, left_ref, right_ref,
    loss_all, ids_ref, idbuf, idrow, gains, wins, wouts, flat, look_out, look_in, tok, layer_in,
    head_out, head_in, stat_out, stat_in, grad_out, grad_in, emb_out, emb_in,
    table_ref, gain_wide, kept, look_pair, grad_pair, send_sem, recv_sem,
):
    devices = sections * replicas
    tokens = replicas * per_dp
    rows_dev, dim = table_ref.shape
    chunks = dim // LANES
    head_ref = right_ref.at[pl.ds(0, tokens)]
    layers = 2 * sections
    scale_in = math.sqrt(dim)
    sec, rep = lax.axis_index("section"), lax.axis_index("dp")
    me = sec * replicas + rep
    offset = me * rows_dev
    all_own = per_dp == sections
    own = sec < per_dp
    own_half = per_dp // 2
    count_half = tokens // 2
    half = sections // 2
    side, partner = sec % 2, sec + 1 - 2 * (sec % 2)
    my_half = rep * own_half + sec // 2
    if not all_own:
        my_half = jnp.where(own, my_half, -1)

    def if_own(body):
        if all_own:
            body()
        else:
            pl.when(own)(body)

    def spread(phase, count, first, target, skip, src, dst):
        def step(i, _):
            at = lax.rem(first + i, count)

            @pl.when(at != skip)
            def _():
                pltpu.make_async_remote_copy(
                    src_ref=src(at),
                    dst_ref=dst,
                    send_sem=send_sem.at[phase],
                    recv_sem=recv_sem.at[phase],
                    device_id=target(at),
                    device_id_type=pl.DeviceIdType.MESH,
                ).start()

            @pl.when(at == skip)
            def _():
                pltpu.make_async_copy(src(at), dst, recv_sem.at[phase]).start()

            return 0

        lax.fori_loop(0, count, step, 0, unroll=8)

    def take(ref, sem):
        pltpu.make_async_copy(ref, ref, sem).wait()

    def any_device(n):
        return (n // replicas, n % replicas)

    def token_device(h):
        return (2 * (h % own_half) + side, h // own_half)

    def side_device(q):
        return (2 * (q // replicas) + side, q % replicas)

    side_me = (sec // 2) * replicas + rep

    def pair_copy(phase, src, dst):
        return pltpu.make_async_remote_copy(
            src_ref=src,
            dst_ref=dst,
            send_sem=send_sem.at[phase],
            recv_sem=recv_sem.at[phase],
            device_id=(partner, rep),
            device_id_type=pl.DeviceIdType.MESH,
        )

    load = pltpu.make_async_copy(table_hbm, table_ref, recv_sem.at[TABLE])
    load.start()
    barrier = pltpu.get_barrier_semaphore()

    def greet(i, _):
        n = lax.rem(me + 1 + i, devices)
        pl.semaphore_signal(
            barrier, inc=1, device_id=any_device(n), device_id_type=pl.DeviceIdType.MESH
        )
        return 0

    lax.fori_loop(0, devices - 1, greet, 0, unroll=8)
    flat[...] = jnp.zeros_like(flat)
    tok[...] = jnp.zeros_like(tok)
    row = lax.broadcasted_iota(jnp.int32, (2 * per_dp, LANES), 0)
    made = jnp.zeros((2 * per_dp, LANES), jnp.int32)
    batches, width = token_ref.shape
    for b in range(batches):
        for w in range(width):
            k = b * width + w
            made = jnp.where(row == k, token_ref[b : b + 1, w : w + 1], made)
            made = jnp.where(row == per_dp + k, target_ref[b : b + 1, w : w + 1], made)
    ids_ref[...] = made
    pl.semaphore_wait(barrier, devices - 1)

    spread(IDS, replicas, rep, lambda d: (sec, d), rep, lambda d: ids_ref, idbuf.at[rep])
    stores = ((GAIN, gain_ref, gains), (WIN, win_ref, wins), (WOUT, wout_ref, wouts))
    for phase, src, dst in stores:
        for i in range(1, half):
            pair = lax.rem(sec // 2 + i, half)
            pltpu.make_async_remote_copy(
                src_ref=src,
                dst_ref=dst.at[side, sec // 2],
                send_sem=send_sem.at[phase],
                recv_sem=recv_sem.at[phase],
                device_id=(2 * pair + side, rep),
                device_id_type=pl.DeviceIdType.MESH,
            ).start()
        pltpu.make_async_copy(src, dst.at[side, sec // 2], recv_sem.at[phase]).start()

    take(idbuf, recv_sem.at[IDS])
    for d in range(replicas):
        for kind in range(2):
            for k in range(per_dp):
                at = (k % 2) * count_half + d * own_half + k // 2
                idrow[kind, pl.ds(at, 1), :] = idbuf[
                    d, pl.ds(kind * per_dp + k, 1), :
                ]
    wide = lambda value: jnp.concatenate([value] * (rows_dev // LANES), axis=1)
    column = lax.broadcasted_iota(jnp.int32, (tokens, rows_dev), 1) + offset
    chosen = jnp.where(wide(idrow[0]) == column, 1.0, 0.0).astype(BF16)
    mask = wide(idrow[1]) == column
    left_ref[pl.ds(tokens, tokens), :] = chosen
    left_ref[pl.ds(2 * tokens, tokens), :] = chosen
    load.wait()

    def scatter(left, phase, out, pair, into):
        for j in range(0, chunks, 2):
            part = jnp.dot(
                left, table_ref[:, j * LANES : (j + 2) * LANES], preferred_element_type=F32
            )
            flat[pl.ds(j, tokens, stride=pad), :] = part[:, :LANES]
            flat[pl.ds(j + 1, tokens, stride=pad), :] = part[:, LANES:]
        mine = pl.ds(pl.multiple_of(side * (count_half * pad), 8), count_half * pad)
        away = pl.ds(pl.multiple_of((1 - side) * (count_half * pad), 8), count_half * pad)
        blocks = (count_half, pad // 8, 8, LANES)
        out[1 - side] = flat[away, :].reshape(blocks).astype(BF16)
        swap = pair_copy(phase + PAIR, out.at[1 - side], pair)
        swap.start()
        swap.wait()
        out[side] = (flat[mine, :].reshape(blocks) + pair[...].astype(F32)).astype(BF16)
        spread(
            phase, count_half, rep * own_half + sec // 2, token_device, my_half,
            lambda h: out.at[side, h], into.at[side_me],
        )

    def total(into):
        return lax.fori_loop(
            0, devices // 2, lambda n, acc: acc + into[n].astype(F32),
            jnp.zeros((pad // 8, 8, LANES), F32),
            unroll=4,
        ).reshape(pad, LANES)

    def spread_rows(values):
        tok[...] = values
        return jnp.concatenate(
            [jnp.broadcast_to(tok[j : j + 1, :], (8, LANES)) for j in range(chunks)], axis=1
        )

    def pack_row(values, out):
        for j in range(chunks):
            tok[j : j + 1, :] = values[0:1, j * LANES : (j + 1) * LANES]
        out[...] = tok[...].reshape(pad // 8, 8, LANES).astype(BF16)

    def norm(x):
        scale = lax.rsqrt(jnp.sum(x * x, axis=1, keepdims=True) * (1.0 / dim) + EPS)
        return x * scale, scale

    def weights(layer):
        s, c = layer % sections, layer // sections
        at = (s % 2, s // 2, c, 0)
        return gain_wide[layer], wins[at].astype(F32), wouts[at].astype(F32)

    def widen(layer, _):
        s, c = layer % sections, layer // sections
        both = gains[s % 2, s // 2].astype(F32)
        picked = jnp.where(c == 0, both[0:1], both[1:2])
        gain_wide[layer] = jnp.broadcast_to(picked, (8, dim))
        return 0

    def gather(phase, block, into):
        if_own(
            lambda: spread(
                phase, devices // 2, side_me, side_device, side_me,
                lambda n: block, into.at[side, my_half],
            )
        )
        take(into.at[side], recv_sem.at[phase])
        relay = pair_copy(phase + PAIR, into.at[side], into.at[side])
        relay.start()
        relay.wait()

    def unpack(into, out):
        flat[...] = into[...].astype(F32).reshape(tokens * pad, LANES)
        for j in range(chunks):
            out(slice(j * LANES, (j + 1) * LANES), flat[pl.ds(j, tokens, stride=pad), :])

    scatter(chosen, LOOK, look_out, look_pair, look_in)
    for phase, _, buf in stores:
        take(buf.at[side], recv_sem.at[phase])
        pltpu.make_async_remote_copy(
            src_ref=buf.at[side],
            dst_ref=buf.at[side],
            send_sem=send_sem.at[phase + RELAY],
            recv_sem=recv_sem.at[phase + RELAY],
            device_id=(partner, rep),
            device_id_type=pl.DeviceIdType.MESH,
        ).start()
    gain_wide[layers] = jnp.broadcast_to(fgain_ref[...].astype(F32)[None], (8, dim))
    take(gains.at[1 - side], recv_sem.at[GAIN + RELAY])
    lax.fori_loop(0, layers, widen, 0)
    for phase, _, buf in stores[1:]:
        take(buf.at[1 - side], recv_sem.at[phase + RELAY])

    def forward():
        take(look_in, recv_sem.at[LOOK])
        x = spread_rows(rounded(total(look_in) * scale_in))

        def layer(index, x):
            layer_in[index] = x
            gain, first, second = weights(index)
            normed, scale = norm(x)
            pre = jnp.sum(rounded(normed * gain) * first, axis=1, keepdims=True)
            hidden = rounded(gelu_tanh(pre))
            kept[index, 0] = jnp.broadcast_to(scale, (8, LANES))
            kept[index, 1] = jnp.broadcast_to(gelu_slope(pre), (8, LANES))
            return rounded(x + jnp.sum(hidden * second, axis=0, keepdims=True))

        x = lax.fori_loop(0, layers, layer, x, unroll=2)
        layer_in[layers] = x
        normed, _ = norm(x)
        pack_row(normed * gain_wide[layers], head_out)

    if_own(forward)
    gather(HEAD, head_out, head_in)

    def store_head(lanes, part):
        right_ref[pl.ds(0, tokens), lanes] = part.astype(BF16)

    unpack(head_in, store_head)

    scores = lax.dot_general(
        head_ref[...], table_ref[...], (((1,), (1,)), ((), ())), preferred_element_type=F32
    )
    squash = jnp.tanh(scores / CAP)
    capped = CAP * squash
    powers = jnp.exp(capped)
    exp_sum = jnp.sum(powers, axis=1, keepdims=True)
    goal = jnp.sum(jnp.where(mask, capped, 0.0), axis=1, keepdims=True)
    groups = tokens // 8
    lane = lax.broadcasted_iota(jnp.int32, (8, LANES), 1)
    tile = jnp.zeros((8, LANES), F32)
    for g in range(groups):
        tile = jnp.where(lane == g, exp_sum[8 * g : 8 * g + 8], tile)
        tile = jnp.where(lane == groups + g, goal[8 * g : 8 * g + 8], tile)
    stat_out[...] = tile
    spread(STAT, devices, me, any_device, me, lambda n: stat_out, stat_in.at[me])
    take(stat_in, recv_sem.at[STAT])
    tile = lax.fori_loop(
        0, devices, lambda n, acc: acc + stat_in[n], jnp.zeros((8, LANES), F32)
    )

    def column_of(first):
        return jnp.concatenate(
            [
                jnp.broadcast_to(tile[:, first + g : first + g + 1], (8, LANES))
                for g in range(groups)
            ],
            axis=0,
        )

    exp_total = column_of(0)
    loss_all[...] = jnp.log(exp_total) - column_of(groups)
    for b in range(batches):
        for w in range(width):
            k = b * width + w
            at = (k % 2) * count_half + rep * own_half + k // 2
            loss_ref[b : b + 1, w : w + 1] = loss_all[pl.ds(at, 1), 0:1]
    score_grad = (
        (powers / wide(exp_total) - jnp.where(mask, 1.0, 0.0)) * (1.0 - squash * squash)
    ).astype(BF16)
    left_ref[pl.ds(0, tokens), :] = score_grad
    scatter(score_grad, GRAD, grad_out, grad_pair, grad_in)

    def backward():
        take(grad_in, recv_sem.at[GRAD])
        grad = spread_rows(total(grad_in)) * gain_wide[layers]

        def back(normed, scale, grad):
            mean = jnp.sum(grad * normed, axis=1, keepdims=True) * (1.0 / dim)
            return scale * (grad - normed * mean)

        dy = rounded(back(*norm(layer_in[layers]), grad))

        def layer(step, dy):
            index = layers - 1 - step
            gain, first, second = weights(index)
            scale = kept[index, 0][:, 0:1]
            normed = layer_in[index] * scale
            hidden_grad = jnp.sum(dy * second, axis=1, keepdims=True)
            pre_grad = rounded(hidden_grad * kept[index, 1][:, 0:1])
            act_grad = jnp.sum(pre_grad * first, axis=0, keepdims=True)
            return rounded(dy + back(normed, scale, act_grad * gain))

        pack_row(lax.fori_loop(0, layers, layer, dy, unroll=2), emb_out)

    if_own(backward)
    gather(EMB, emb_out, emb_in)

    def store_emb(lanes, part):
        part = part * scale_in
        high = part.astype(BF16)
        right_ref[pl.ds(tokens, tokens), lanes] = high
        right_ref[pl.ds(2 * tokens, tokens), lanes] = (part - high.astype(F32)).astype(BF16)

    unpack(emb_in, store_emb)

    take(idbuf.at[pl.ds(0, replicas - 1)], send_sem.at[IDS])
    for phase, _, buf in stores:
        if half > 1:
            take(buf.at[0, pl.ds(0, half - 1)], send_sem.at[phase])
        take(buf.at[0], send_sem.at[phase + RELAY])
    take(stat_in.at[pl.ds(0, devices - 1)], send_sem.at[STAT])

    def owned():
        take(look_pair.at[pl.ds(0, count_half - 1)], send_sem.at[LOOK])
        take(grad_pair.at[pl.ds(0, count_half - 1)], send_sem.at[GRAD])
        take(look_in.at[pl.ds(0, devices // 2 - 1)], send_sem.at[HEAD])
        take(grad_in.at[pl.ds(0, devices // 2 - 1)], send_sem.at[EMB])

    if_own(owned)
    if not all_own:

        @pl.when(jnp.logical_not(own))
        def _():
            take(look_pair, send_sem.at[LOOK])
            take(grad_pair, send_sem.at[GRAD])


def table_kernel(left_ref, right_ref, out_ref):
    over = (((0,), (0,)), ((), ()))
    step = out_ref.shape[1]
    lanes = pl.ds(pl.multiple_of(pl.program_id(0) * step, LANES), step)
    out_ref[...] = lax.dot_general(
        left_ref[...], right_ref[:, lanes], over, preferred_element_type=F32
    ).astype(BF16)


def per_device(token_ids, target_ids, table, norm_gain, w_in, w_out, final_gain):
    sections, replicas = lax.axis_size("section"), lax.axis_size("dp")
    batches, width = token_ids.shape
    rows_dev, dim = table.shape
    rank = w_in.shape[2]
    per_dp = batches * width
    tokens = replicas * per_dp
    devices = sections * replicas
    chunks = dim // LANES
    pad = (chunks + 7) // 8 * 8
    assert per_dp <= sections and tokens % 8 == 0
    assert chunks % 2 == 0 and rows_dev % LANES == 0
    assert per_dp % 2 == 0 and sections % 2 == 0
    block = (pad // 8, 8, LANES)
    vmem = pl.BlockSpec(memory_space=pltpu.VMEM)
    hbm = pl.BlockSpec(memory_space=pltpu.HBM)
    token_loss, left, right = pl.pallas_call(
        functools.partial(cascade, sections, replicas, per_dp, pad),
        out_shape=(
            jax.ShapeDtypeStruct((batches, width), F32),
            jax.ShapeDtypeStruct((3 * tokens, rows_dev), BF16),
            jax.ShapeDtypeStruct((3 * tokens, dim), BF16),
        ),
        in_specs=[vmem, vmem, hbm, vmem, vmem, hbm, hbm],
        out_specs=(vmem,) * 3,
        scratch_shapes=[
            pltpu.VMEM((tokens, LANES), F32),
            pltpu.VMEM((2 * per_dp, LANES), jnp.int32),
            pltpu.VMEM((replicas, 2 * per_dp, LANES), jnp.int32),
            pltpu.VMEM((2, tokens, LANES), jnp.int32),
            pltpu.VMEM((2, sections // 2, 2, dim), BF16),
            pltpu.VMEM((2, sections // 2, 2, 1, rank, dim), BF16),
            pltpu.VMEM((2, sections // 2, 2, 1, rank, dim), BF16),
            pltpu.VMEM((tokens * pad, LANES), F32),
            pltpu.VMEM((2, tokens // 2) + block, BF16),
            pltpu.VMEM((devices // 2,) + block, BF16),
            pltpu.VMEM((pad, LANES), F32),
            pltpu.VMEM((2 * sections + 1, 8, dim), F32),
            pltpu.VMEM(block, BF16),
            pltpu.VMEM((2, tokens // 2) + block, BF16),
            pltpu.VMEM((8, LANES), F32),
            pltpu.VMEM((devices, 8, LANES), F32),
            pltpu.VMEM((2, tokens // 2) + block, BF16),
            pltpu.VMEM((devices // 2,) + block, BF16),
            pltpu.VMEM(block, BF16),
            pltpu.VMEM((2, tokens // 2) + block, BF16),
            pltpu.VMEM((rows_dev, dim), BF16),
            pltpu.VMEM((2 * sections + 1, 8, dim), F32),
            pltpu.VMEM((2 * sections, 2, 8, LANES), F32),
            pltpu.VMEM((tokens // 2,) + block, BF16),
            pltpu.VMEM((tokens // 2,) + block, BF16),
            pltpu.SemaphoreType.DMA((19,)),
            pltpu.SemaphoreType.DMA((19,)),
        ],
        compiler_params=pltpu.CompilerParams(
            collective_id=0, has_side_effects=True, vmem_limit_bytes=63400000
        ),
        name="cascade",
    )(token_ids, target_ids, table, norm_gain[:, 0], final_gain, w_in, w_out)
    step = dim // 3
    table_grad = pl.pallas_call(
        table_kernel,
        out_shape=jax.ShapeDtypeStruct((rows_dev, dim), BF16),
        grid=(dim // step,),
        in_specs=[vmem, vmem],
        out_specs=pl.BlockSpec((rows_dev, step), lambda i: (0, i)),
        name="table_grad",
    )(left, right)
    return (token_loss, table_grad)


def solution(mesh):
    return jax.shard_map(
        per_device,
        mesh=mesh,
        in_specs=(
            P(None, "dp"),
            P(None, "dp"),
            P(("section", "dp"), None),
            P(None, "section", None),
            P(None, "section", None, None),
            P(None, "section", None, None),
            P(),
        ),
        out_specs=(P(None, "dp"), P(("section", "dp"), None)),
        check_vma=False,
    )
```
